32 devices in a mesh: dp: 8 (over y, x, core), tensor: 4 (over z).
Axes of the slice: x: 2, y: 2, z: 4, core: 2. Of those that a mesh axis runs over, the one named last changes fastest.
Arguments:
- tokens: bfloat16 [16384, 1024], P(('dp', 'tensor')), may hold values from -6 to 6
- lengths: int32 [32], P('dp'), may hold values from 1 to 512, 10240 in all
- w_qkv: bfloat16 [1024, 3, 1024], P('dp', None, 'tensor'), may hold values from -0.1875 to 0.1875
- b_qv: bfloat16 [2, 1024], P(None, 'tensor'), may hold values from -3 to 3
- w_out: bfloat16 [1024, 1024], P('dp', 'tensor'), may hold values from -1 to 1
- b_out: bfloat16 [1024], replicated, may hold values from -3 to 3
- gain_one: bfloat16 [1024], replicated, may hold values from 0.5 to 1.5
- shift_one: bfloat16 [1024], replicated, may hold values from -3 to 3
- w_in: bfloat16 [1024, 4096], P('dp', 'tensor'), may hold values from -0.1875 to 0.1875
- b_in: bfloat16 [4096], P('tensor'), may hold values from -3 to 3
- w_back: bfloat16 [1024, 4096], P('dp', 'tensor'), may hold values from -0.09375 to 0.09375
- b_back: bfloat16 [1024], replicated, may hold values from -3 to 3
- gain_two: bfloat16 [1024], replicated, may hold values from 0.5 to 1.5
- shift_two: bfloat16 [1024], replicated, may hold values from -3 to 3
- cotangent: bfloat16 [16384, 1024], P(('dp', 'tensor')), may hold values from -6 to 6
Outputs:
- output: bfloat16 [16384, 1024], P(('dp', 'tensor'))
- grad_tokens: float32 [16384, 1024], P(('dp', 'tensor'))
- grad_w_qkv: float32 [1024, 3, 1024], P('dp', None, 'tensor')
- grad_b_qv: float32 [2, 1024], P(None, 'tensor')
- grad_w_out: float32 [1024, 1024], P('dp', 'tensor')
- grad_b_out: float32 [1024], replicated
- grad_gain_one: float32 [1024], replicated
- grad_shift_one: float32 [1024], replicated
- grad_w_in: float32 [1024, 4096], P('dp', 'tensor')
- grad_b_in: float32 [4096], P('tensor')
- grad_w_back: float32 [1024, 4096], P('dp', 'tensor')
- grad_b_back: float32 [1024], replicated
- grad_gain_two: float32 [1024], replicated
- grad_shift_two: float32 [1024], replicated
The draws below stay inside these ranges and needn't reach their ends.
Inputs may be any that keep to these rules, and one draw needn't show every extreme that they name: `lengths`: the valid tokens of each sequence; all of them sum to 10240 and the largest is 512.
All inputs are finite; a program needn't handle non-finite values. No bound on the sum of `lengths` on one device may be relied on, other than what follows from the above.
Results may differ from the reference program's by a relative error of at most 0.018.
Values may be sent and summed in bfloat16 or wider, within the bound.
A program may use at most 128 MiB of HBM per device.

```python
import math
import jax
import jax.numpy as jnp
import numpy as np
from jax import lax

D = 1024
H = 16
FF = 4096
LEN = 512
SEQ_GRP = 4
HD = 64
NSEQ = 32
TOKENS = 16384
N_DP = 8
N_TENSOR = 4


def level_of(key, shape, cuts, least, high):
    factor_of, own = 1.0, jax.random.fold_in(key, 6)
    for axis_at, shards_of in cuts:
        draws = jnp.exp(jax.random.uniform(jax.random.fold_in(own, axis_at), (shards_of,), jnp.float32, least / len(cuts), high / len(cuts)))
        factor_of = factor_of * jnp.repeat(draws, shape[axis_at] // shards_of).reshape([-1 if axis == axis_at else 1 for axis in range(len(shape))])
    return factor_of


def profile(count, total, bound, lean):
    portions = [(1 << 20) // math.isqrt(grade ** lean) + 1 for grade in range(2, count + 1)]
    spare, holding = total - bound - (count - 1), [1] * (count - 1)
    while spare > 0:
        movable = [i for i in range(count - 1) if holding[i] < bound]
        whole, budget = sum([portions[i] for i in movable]), spare
        for i in movable:
            extra = min(bound - holding[i], max(1, budget * portions[i] // whole), spare)
            holding[i] = holding[i] + extra
            spare = spare - extra
    return np.array([bound] + holding)


def uneven(own_key, count, total, bound, slope):
    if count == 2:
        one = jax.random.randint(own_key, (), max(1, total - bound), min(bound, total - 1) + 1)
        return jnp.stack([one, total - one])
    sizes = jnp.asarray(profile(count, total, bound, slope), jnp.int32)
    twos = (count - 1) // 2
    source_of, receiver = sizes[1:1 + 2 * twos:2], sizes[2:2 + 2 * twos:2]
    margin = jnp.minimum(source_of - 1, bound - receiver)
    shifted = jax.random.randint(jax.random.fold_in(own_key, 1), (twos,), 0, 1 << 20) % (margin + 1)
    sizes = sizes.at[1:1 + 2 * twos:2].set(source_of - shifted).at[2:2 + 2 * twos:2].set(receiver + shifted)
    return sizes[jax.random.permutation(jax.random.fold_in(own_key, 2), count)]


def gaussian(key, dims, scale, most, split=(), held_as=jnp.bfloat16):
    array = jax.random.normal(key, dims, jnp.float32) * scale
    if len(split) > 0:
        array = level_of(key, dims, split, -0.22, 0.18) * array
    return jnp.clip(array, min=-most, max=most).astype(held_as)


def setup_inputs(seed: int = 0) -> dict:
    key_of = jax.random.split(jax.random.key(seed), 16)
    tokens = gaussian(key_of[0], (TOKENS, D), 1.0, 6.0, ((0, 32),))
    lengths = uneven(key_of[1], NSEQ, NSEQ * LEN * 5 // 8, LEN, 2).astype(jnp.int32)
    w_qkv = gaussian(key_of[2], (D, 3, D), D ** -0.5, 0.1875, ((0, 8), (2, 4)))
    b_qv = gaussian(key_of[3], (2, D), 0.5, 3.0, ((1, 4),))
    w_out = gaussian(key_of[4], (D, D), (D // 32) ** -0.5, 1.0, ((0, 8), (1, 4)))
    b_out = gaussian(key_of[5], (D,), 0.5, 3.0)
    gain_one = jnp.clip(1.0 + 0.1 * jax.random.normal(key_of[6], (D,), jnp.float32), 0.5, 1.5).astype(jnp.bfloat16)
    shift_one = gaussian(key_of[7], (D,), 0.5, 3.0)
    w_in = gaussian(key_of[8], (D, FF), D ** -0.5, 0.1875, ((0, 8), (1, 4)))
    b_in = gaussian(key_of[9], (FF,), 0.5, 3.0, ((0, 4),))
    w_back = gaussian(key_of[10], (D, FF), FF ** -0.5, 0.09375, ((0, 8), (1, 4)))
    b_back = gaussian(key_of[11], (D,), 0.5, 3.0)
    gain_two = jnp.clip(1.0 + 0.1 * jax.random.normal(key_of[12], (D,), jnp.float32), 0.5, 1.5).astype(jnp.bfloat16)
    shift_two = gaussian(key_of[13], (D,), 0.5, 3.0)
    cotangent = gaussian(key_of[14], (TOKENS, D), 1.0, 6.0, ((0, 32),))
    return dict(tokens=tokens, lengths=lengths, w_qkv=w_qkv, b_qv=b_qv, w_out=w_out, b_out=b_out, gain_one=gain_one, shift_one=shift_one, w_in=w_in, b_in=b_in, w_back=w_back, b_back=b_back, gain_two=gain_two, shift_two=shift_two, cotangent=cotangent)


EPS = 1e-05
MASKED = -1000000000.0
HIGH = lax.Precision.HIGHEST

@jax.custom_vjp
def low(v):
    return lax.optimization_barrier(v.astype(jnp.bfloat16)).astype(jnp.float32)

@jax.custom_vjp
def low_back(v):
    return v

def low_keep(v):
    return (low(v), None)

def low_pass(kept, grad):
    return (grad,)

def back_keep(v):
    return (v, None)

def back_low(kept, grad):
    return (low(grad),)
low.defvjp(low_keep, low_pass)
low_back.defvjp(back_keep, back_low)

def layer_norm(values, gain, shift):
    centred = values - lax.optimization_barrier(jnp.mean(values, axis=-1, keepdims=True))
    variance = lax.optimization_barrier(jnp.mean(centred * centred, axis=-1, keepdims=True))
    return centred * lax.rsqrt(variance + EPS) * gain + shift

def attend(inputs):
    query_seq, key_seq, value_seq, keep_seq = inputs
    scores = jnp.einsum('qhe,khe->hqk', query_seq, key_seq, precision=HIGH) * HD ** (-0.5)
    scores = low_back(scores)
    scores = jnp.where(keep_seq[None, None, :], scores, MASKED)
    probs = low(jax.nn.softmax(scores, axis=-1))
    return jnp.einsum('hqk,khe->qhe', probs, value_seq, precision=HIGH)

def group_forward(params, rows, keep):
    w_qkv, b_qv, w_out, b_out, gain_one, shift_one, w_in, b_in, w_back, b_back, gain_two, shift_two = params
    projected = jnp.einsum('rd,dcf->rcf', rows, w_qkv, precision=HIGH)
    queries = low_back(low(projected[:, 0] + b_qv[0]))
    keyset = low_back(low(projected[:, 1]))
    valueset = low_back(low(projected[:, 2] + b_qv[1]))
    shape4 = (SEQ_GRP, LEN, H, HD)
    mixed = lax.map(jax.checkpoint(attend), (queries.reshape(shape4), keyset.reshape(shape4), valueset.reshape(shape4), keep))
    attended = low_back(low(mixed.reshape(SEQ_GRP * LEN, D)))
    pieces = attended.reshape(SEQ_GRP * LEN, N_TENSOR, D // N_TENSOR)
    weight_pieces = w_out.reshape(D, N_TENSOR, D // N_TENSOR)
    partial_one = low(jnp.einsum('rtc,otc->rto', pieces, weight_pieces, precision=HIGH))
    branch_one = low_back(lax.optimization_barrier(jnp.sum(partial_one, axis=1)) + b_out)
    hidden = layer_norm(rows + branch_one, gain_one, shift_one)
    pre_act = low_back(jnp.dot(low(hidden), w_in, precision=HIGH) + b_in)
    activated = low(jax.nn.gelu(pre_act, approximate=False))
    act_pieces = activated.reshape(SEQ_GRP * LEN, N_TENSOR, FF // N_TENSOR)
    back_pieces = w_back.reshape(D, N_TENSOR, FF // N_TENSOR)
    partial_two = low(jnp.einsum('rtc,otc->rto', act_pieces, back_pieces, precision=HIGH))
    branch_two = low_back(lax.optimization_barrier(jnp.sum(partial_two, axis=1)) + b_back)
    return layer_norm(hidden + branch_two, gain_two, shift_two)

def add_pair(first, second):
    return first + second

def reference(tokens, lengths, w_qkv, b_qv, w_out, b_out, gain_one, shift_one, w_in, b_in, w_back, b_back, gain_two, shift_two, cotangent):
    params = tuple((item.astype(jnp.float32) for item in (w_qkv, b_qv, w_out, b_out, gain_one, shift_one, w_in, b_in, w_back, b_back, gain_two, shift_two)))
    rows_all = tokens.astype(jnp.float32).reshape(N_DP, SEQ_GRP * LEN, D)
    grads_all = cotangent.astype(jnp.float32).reshape(N_DP, SEQ_GRP * LEN, D)
    positions = jnp.arange(LEN).astype(jnp.int32)
    keep_all = positions[None, None, :] < lengths.astype(jnp.int32).reshape(N_DP, SEQ_GRP)[:, :, None]

    def step(carry, inputs):
        rows, keep, grad_out = inputs

        def forward(weights, values):
            return group_forward(weights, values, keep)
        result, pullback = jax.vjp(forward, params, rows)
        grad_params, grad_rows = pullback(grad_out)
        return (jax.tree.map(add_pair, carry, grad_params), (result, grad_rows))
    zeros = jax.tree.map(jnp.zeros_like, params)
    totals, (outputs, grad_rows) = lax.scan(step, zeros, (rows_all, keep_all, grads_all))
    return (outputs.reshape(TOKENS, D).astype(jnp.bfloat16), grad_rows.reshape(TOKENS, D), totals[0], totals[1], totals[2], totals[3], totals[4], totals[5], totals[6], totals[7], totals[8], totals[9], totals[10], totals[11])
```

```python
import functools

import jax
import jax.numpy as jnp
from jax import lax
from jax.experimental import pallas as pl
from jax.experimental.pallas import tpu as pltpu
from jax.sharding import PartitionSpec as P

H = 16
EPS = 1e-05
MASKED = -1000000000.0
SQRT_HALF = 0.7071067811865476
INV_ROOT_TAU = 0.3989422804014327
ROWS_NT = (((1,), (1,)), ((), ()))
ROWS_TN = (((0,), (0,)), ((), ()))
ALL = ("tensor", "dp")


def dot(a, b):
    return jnp.dot(a, b, preferred_element_type=jnp.float32)


def dot_nt(a, b):
    return lax.dot_general(a, b, ROWS_NT, preferred_element_type=jnp.float32)


def dot_tn(a, b):
    return lax.dot_general(a, b, ROWS_TN, preferred_element_type=jnp.float32)


def normalize(values, gain, shift):
    centre = values - jnp.mean(values, axis=-1, keepdims=True)
    inverse = lax.rsqrt(jnp.mean(centre * centre, axis=-1, keepdims=True) + EPS)
    scaled = centre * inverse
    return (scaled * gain + shift, scaled, inverse)


def norm_back(grad_out, scaled, inverse, gain):
    grad_scaled = grad_out * gain
    inner = jnp.mean(grad_scaled, axis=-1, keepdims=True)
    along = jnp.mean(grad_scaled * scaled, axis=-1, keepdims=True)
    return inverse * (grad_scaled - inner - scaled * along)


def softmax_of(query, key, limit, scale):
    scores = dot_nt(query, key) * scale
    column = lax.broadcasted_iota(jnp.int32, scores.shape, 1)
    scores = jnp.where(column < limit, scores, MASKED)
    expo = jnp.exp(scores - jnp.max(scores, axis=-1, keepdims=True))
    return expo * (1.0 / jnp.sum(expo, axis=-1, keepdims=True))


def attend_kernel(width, head, seq_len, limit_ref, qkv_ref, out_ref):
    limit = limit_ref[pl.program_id(0)]
    for at in range(width // head):
        low = at * head
        query = qkv_ref[:, low : low + head]
        key = qkv_ref[:, width + low : width + low + head]
        value = qkv_ref[:, 2 * width + low : 2 * width + low + head]
        probs = softmax_of(query, key, limit, head**-0.5).astype(jnp.bfloat16)
        out_ref[:, low : low + head] = dot(probs, value).astype(jnp.bfloat16)


def attend_back_kernel(width, head, seq_len, limit_ref, qkv_ref, grad_ref, out_ref):
    limit = limit_ref[pl.program_id(0)]
    scale = head**-0.5
    for at in range(width // head):
        low = at * head
        query = qkv_ref[:, low : low + head]
        key = qkv_ref[:, width + low : width + low + head]
        value = qkv_ref[:, 2 * width + low : 2 * width + low + head]
        grad = grad_ref[:, low : low + head]
        probs = softmax_of(query, key, limit, scale)
        grad_probs = dot_nt(grad, value)
        inner = jnp.sum(grad_probs * probs, axis=-1, keepdims=True)
        grad_scores = (probs * (grad_probs - inner)).astype(jnp.bfloat16)
        out_ref[:, low : low + head] = (dot(grad_scores, key) * scale).astype(jnp.bfloat16)
        out_ref[:, width + low : width + low + head] = (dot_tn(grad_scores, query) * scale).astype(
            jnp.bfloat16
        )
        out_ref[:, 2 * width + low : 2 * width + low + head] = dot_tn(
            probs.astype(jnp.bfloat16), grad
        ).astype(jnp.bfloat16)


def attend(limits, qkv, seq_len, width, head):
    rows = qkv.shape[0]
    groups = qkv.shape[1] // (3 * width)
    return pl.pallas_call(
        functools.partial(attend_kernel, width, head, seq_len),
        grid_spec=pltpu.PrefetchScalarGridSpec(
            num_scalar_prefetch=1,
            grid=(rows // seq_len, groups),
            in_specs=[pl.BlockSpec((seq_len, 3 * width), lambda s, g, lim: (s, g))],
            out_specs=pl.BlockSpec((seq_len, width), lambda s, g, lim: (s, g)),
        ),
        out_shape=jax.ShapeDtypeStruct((rows, groups * width), jnp.bfloat16),
        cost_estimate=pl.CostEstimate(
            flops=16 * rows * seq_len * groups * width,
            bytes_accessed=8 * rows * groups * width,
            transcendentals=rows * seq_len * groups * width // head,
        ),
    )(limits, qkv)


def attend_back(limits, qkv, grad, seq_len, width, head):
    rows = qkv.shape[0]
    groups = qkv.shape[1] // (3 * width)
    return pl.pallas_call(
        functools.partial(attend_back_kernel, width, head, seq_len),
        grid_spec=pltpu.PrefetchScalarGridSpec(
            num_scalar_prefetch=1,
            grid=(rows // seq_len, groups),
            in_specs=[
                pl.BlockSpec((seq_len, 3 * width), lambda s, g, lim: (s, g)),
                pl.BlockSpec((seq_len, width), lambda s, g, lim: (s, g)),
            ],
            out_specs=pl.BlockSpec((seq_len, 3 * width), lambda s, g, lim: (s, g)),
        ),
        out_shape=jax.ShapeDtypeStruct(qkv.shape, jnp.bfloat16),
        cost_estimate=pl.CostEstimate(
            flops=40 * rows * seq_len * groups * width,
            bytes_accessed=14 * rows * groups * width,
            transcendentals=rows * seq_len * groups * width // head,
        ),
    )(limits, qkv, grad)


def gather(weight):
    return lax.all_gather(weight, ALL, axis=0, tiled=True)


def scatter(parts):
    owners = lax.axis_size("dp")
    split = [
        part.astype(jnp.bfloat16).reshape(owners, part.shape[0] // owners, part.shape[1])
        for part in parts
    ]
    stacked = jnp.stack(split, axis=1).reshape(-1, parts[0].shape[1])
    own = lax.psum_scatter(stacked, "dp", scatter_dimension=0, tiled=True)
    return lax.psum_scatter(own, "tensor", scatter_dimension=0, tiled=True).astype(jnp.float32)


def body(
    tokens,
    lengths,
    w_qkv,
    b_qv,
    w_out,
    b_out,
    gain_one,
    shift_one,
    w_in,
    b_in,
    w_back,
    b_back,
    gain_two,
    shift_two,
    cotangent,
):
    groups = lax.axis_size("tensor")
    slot = lax.axis_index("tensor")
    rows, width = tokens.shape
    seq_len = rows * groups // lengths.shape[0]
    own_seqs = rows // seq_len
    part = w_qkv.shape[2]
    hidden_part = w_in.shape[1]
    head = width // H
    limits = lax.dynamic_slice_in_dim(lengths, slot * own_seqs, own_seqs, 0)

    def split(full):
        return [full[g * width : (g + 1) * width] for g in range(groups)]

    full_qkv = split(gather(w_qkv.reshape(w_qkv.shape[0], 3 * part)))
    full_out = split(gather(w_out))
    full_in = split(gather(w_in))
    full_back = split(gather(w_back))
    bias_qv_all = lax.all_gather(b_qv, "tensor", axis=1, tiled=True).astype(jnp.float32)
    bias_in_all = lax.all_gather(b_in, "tensor", axis=0, tiled=True).astype(jnp.float32)

    qkv_parts = []
    for g in range(groups):
        bias = bias_qv_all[:, g * part : (g + 1) * part]
        bias = jnp.concatenate([bias[0], jnp.zeros((part,), jnp.float32), bias[1]])
        qkv_parts.append((dot(tokens, full_qkv[g]) + bias).astype(jnp.bfloat16))
    qkv = jnp.concatenate(qkv_parts, axis=1)
    attended = attend(limits, qkv, seq_len, part, head)

    attn = sum(
        dot_nt(attended[:, g * part : (g + 1) * part], full_out[g]) for g in range(groups)
    )
    residual_one = tokens.astype(jnp.float32) + attn + b_out.astype(jnp.float32)
    gain_a = gain_one.astype(jnp.float32)
    hidden, scaled_one, inverse_one = normalize(residual_one, gain_a, shift_one.astype(jnp.float32))
    hidden_b = hidden.astype(jnp.bfloat16)

    pre_act = []
    activated = []
    for g in range(groups):
        pre = dot(hidden_b, full_in[g]) + bias_in_all[g * hidden_part : (g + 1) * hidden_part]
        pre_act.append(pre)
        activated.append(jax.nn.gelu(pre, approximate=False).astype(jnp.bfloat16))
    ffn = sum(dot_nt(activated[g], full_back[g]) for g in range(groups))
    residual_two = hidden + ffn + b_back.astype(jnp.float32)
    gain_b = gain_two.astype(jnp.float32)
    output, scaled_two, inverse_two = normalize(residual_two, gain_b, shift_two.astype(jnp.float32))

    grad_out = cotangent.astype(jnp.float32)
    grad_gain_two = jnp.sum(grad_out * scaled_two, axis=0)
    grad_shift_two = jnp.sum(grad_out, axis=0)
    grad_res_two = norm_back(grad_out, scaled_two, inverse_two, gain_b)
    grad_ffn = grad_res_two.astype(jnp.bfloat16)
    grad_b_back = jnp.sum(grad_ffn.astype(jnp.float32), axis=0)
    owner_back = scatter([dot_tn(grad_ffn, activated[g]) for g in range(groups)])

    grad_pre = []
    for g in range(groups):
        pre = pre_act[g]
        slope = 0.5 * (1.0 + lax.erf(pre * SQRT_HALF)) + pre * INV_ROOT_TAU * jnp.exp(
            -0.5 * pre * pre
        )
        grad_pre.append((dot(grad_ffn, full_back[g]) * slope).astype(jnp.bfloat16))
    grad_b_in = jnp.concatenate([jnp.sum(one.astype(jnp.float32), axis=0) for one in grad_pre])
    owner_in = scatter([dot_tn(hidden_b, grad_pre[g]) for g in range(groups)])
    grad_hidden = grad_res_two + sum(dot_nt(grad_pre[g], full_in[g]) for g in range(groups))
    grad_gain_one = jnp.sum(grad_hidden * scaled_one, axis=0)
    grad_shift_one = jnp.sum(grad_hidden, axis=0)
    grad_res_one = norm_back(grad_hidden, scaled_one, inverse_one, gain_a)
    grad_attn = grad_res_one.astype(jnp.bfloat16)
    grad_b_out = jnp.sum(grad_attn.astype(jnp.float32), axis=0)
    owner_out = scatter(
        [dot_tn(grad_attn, attended[:, g * part : (g + 1) * part]) for g in range(groups)]
    )
    grad_mixed = jnp.concatenate(
        [dot(grad_attn, full_out[g]).astype(jnp.bfloat16) for g in range(groups)], axis=1
    )
    grad_qkv = attend_back(limits, qkv, grad_mixed, seq_len, part, head)
    grad_parts = [grad_qkv[:, g * 3 * part : (g + 1) * 3 * part] for g in range(groups)]
    owner_qkv = scatter([dot_tn(tokens, grad_parts[g]) for g in range(groups)])
    grad_tokens = grad_res_one + sum(dot_nt(grad_parts[g], full_qkv[g]) for g in range(groups))
    grad_sums = jnp.sum(grad_qkv.astype(jnp.float32), axis=0).reshape(groups, 3, part)
    grad_b_qv = jnp.stack([grad_sums[:, 0].reshape(width), grad_sums[:, 2].reshape(width)])

    summed = lax.psum(
        (
            grad_b_qv,
            grad_b_in,
            grad_b_out,
            grad_gain_one,
            grad_shift_one,
            grad_b_back,
            grad_gain_two,
            grad_shift_two,
        ),
        ("dp", "tensor"),
    )
    owner_b_qv = lax.dynamic_slice_in_dim(summed[0], slot * part, part, 1)
    owner_b_in = lax.dynamic_slice_in_dim(summed[1], slot * hidden_part, hidden_part, 0)
    return (
        output.astype(jnp.bfloat16),
        grad_tokens,
        owner_qkv.reshape(w_qkv.shape),
        owner_b_qv,
        owner_out,
        summed[2],
        summed[3],
        summed[4],
        owner_in,
        owner_b_in,
        owner_back,
        summed[5],
        summed[6],
        summed[7],
    )


def solution(mesh):
    in_specs = (
        P(("dp", "tensor"), None),
        P("dp"),
        P("dp", None, "tensor"),
        P(None, "tensor"),
        P("dp", "tensor"),
        P(),
        P(),
        P(),
        P("dp", "tensor"),
        P("tensor"),
        P("dp", "tensor"),
        P(),
        P(),
        P(),
        P(("dp", "tensor"), None),
    )
    out_specs = (
        P(("dp", "tensor"), None),
        P(("dp", "tensor"), None),
        P("dp", None, "tensor"),
        P(None, "tensor"),
        P("dp", "tensor"),
        P(),
        P(),
        P(),
        P("dp", "tensor"),
        P("tensor"),
        P("dp", "tensor"),
        P(),
        P(),
        P(),
    )
    return jax.shard_map(body, mesh=mesh, in_specs=in_specs, out_specs=out_specs, check_vma=False)
```

```python
import functools

import jax
import jax.numpy as jnp
from jax import lax
from jax.experimental import pallas as pl
from jax.experimental.pallas import tpu as pltpu
from jax.sharding import PartitionSpec as P

H = 16
EPS = 1e-05
MASKED = -1000000000.0
SQRT_HALF = 0.7071067811865476
INV_ROOT_TAU = 0.3989422804014327
ROWS_NT = (((1,), (1,)), ((), ()))
ROWS_TN = (((0,), (0,)), ((), ()))


def dot(a, b):
    return jnp.dot(a, b, preferred_element_type=jnp.float32)


def dot_nt(a, b):
    return lax.dot_general(a, b, ROWS_NT, preferred_element_type=jnp.float32)


def dot_tn(a, b):
    return lax.dot_general(a, b, ROWS_TN, preferred_element_type=jnp.float32)


def normalize(values, gain, shift):
    centre = values - jnp.mean(values, axis=-1, keepdims=True)
    inverse = lax.rsqrt(jnp.mean(centre * centre, axis=-1, keepdims=True) + EPS)
    scaled = centre * inverse
    return (scaled * gain + shift, scaled, inverse)


def norm_back(grad_out, scaled, inverse, gain):
    grad_scaled = grad_out * gain
    inner = jnp.mean(grad_scaled, axis=-1, keepdims=True)
    along = jnp.mean(grad_scaled * scaled, axis=-1, keepdims=True)
    return inverse * (grad_scaled - inner - scaled * along)


def softmax_of(query, key, limit, scale):
    scores = dot_nt(query, key) * scale
    column = lax.broadcasted_iota(jnp.int32, scores.shape, 1)
    scores = jnp.where(column < limit, scores, MASKED)
    expo = jnp.exp(scores - jnp.max(scores, axis=-1, keepdims=True))
    return expo * (1.0 / jnp.sum(expo, axis=-1, keepdims=True))


def attend_kernel(width, head, seq_len, limit_ref, qkv_ref, out_ref):
    limit = limit_ref[pl.program_id(0)]
    for at in range(width // head):
        low = at * head
        query = qkv_ref[:, low : low + head]
        key = qkv_ref[:, width + low : width + low + head]
        value = qkv_ref[:, 2 * width + low : 2 * width + low + head]
        probs = softmax_of(query, key, limit, head**-0.5).astype(jnp.bfloat16)
        out_ref[:, low : low + head] = dot(probs, value).astype(jnp.bfloat16)


def attend_back_kernel(width, head, seq_len, limit_ref, qkv_ref, grad_ref, out_ref):
    limit = limit_ref[pl.program_id(0)]
    scale = head**-0.5
    for at in range(width // head):
        low = at * head
        query = qkv_ref[:, low : low + head]
        key = qkv_ref[:, width + low : width + low + head]
        value = qkv_ref[:, 2 * width + low : 2 * width + low + head]
        grad = grad_ref[:, low : low + head]
        probs = softmax_of(query, key, limit, scale)
        grad_probs = dot_nt(grad, value)
        inner = jnp.sum(grad_probs * probs, axis=-1, keepdims=True)
        grad_scores = (probs * (grad_probs - inner)).astype(jnp.bfloat16)
        out_ref[:, low : low + head] = (dot(grad_scores, key) * scale).astype(jnp.bfloat16)
        out_ref[:, width + low : width + low + head] = (dot_tn(grad_scores, query) * scale).astype(
            jnp.bfloat16
        )
        out_ref[:, 2 * width + low : 2 * width + low + head] = dot_tn(
            probs.astype(jnp.bfloat16), grad
        ).astype(jnp.bfloat16)


def attend(limits, qkv, seq_len, width, head):
    rows = qkv.shape[0]
    groups = qkv.shape[1] // (3 * width)
    return pl.pallas_call(
        functools.partial(attend_kernel, width, head, seq_len),
        grid_spec=pltpu.PrefetchScalarGridSpec(
            num_scalar_prefetch=1,
            grid=(rows // seq_len, groups),
            in_specs=[pl.BlockSpec((seq_len, 3 * width), lambda s, g, lim: (s, g))],
            out_specs=pl.BlockSpec((seq_len, width), lambda s, g, lim: (s, g)),
        ),
        out_shape=jax.ShapeDtypeStruct((rows, groups * width), jnp.bfloat16),
        cost_estimate=pl.CostEstimate(
            flops=16 * rows * seq_len * groups * width,
            bytes_accessed=8 * rows * groups * width,
            transcendentals=rows * seq_len * groups * width // head,
        ),
    )(limits, qkv)


def attend_back(limits, qkv, grad, seq_len, width, head):
    rows = qkv.shape[0]
    groups = qkv.shape[1] // (3 * width)
    return pl.pallas_call(
        functools.partial(attend_back_kernel, width, head, seq_len),
        grid_spec=pltpu.PrefetchScalarGridSpec(
            num_scalar_prefetch=1,
            grid=(rows // seq_len, groups),
            in_specs=[
                pl.BlockSpec((seq_len, 3 * width), lambda s, g, lim: (s, g)),
                pl.BlockSpec((seq_len, width), lambda s, g, lim: (s, g)),
            ],
            out_specs=pl.BlockSpec((seq_len, 3 * width), lambda s, g, lim: (s, g)),
        ),
        out_shape=jax.ShapeDtypeStruct(qkv.shape, jnp.bfloat16),
        cost_estimate=pl.CostEstimate(
            flops=40 * rows * seq_len * groups * width,
            bytes_accessed=14 * rows * groups * width,
            transcendentals=rows * seq_len * groups * width // head,
        ),
    )(limits, qkv, grad)


def bit_orders():
    bits = lax.axis_size("dp").bit_length() - 1
    outer = list(range(1, bits))
    return outer, outer[::-1]


def exchange(value, bit):
    size = lax.axis_size("dp")
    return lax.ppermute(value, "dp", [(i, i ^ (1 << bit)) for i in range(size)])


def rank(bit):
    return lax.axis_size("dp") if bit == 0 else bit


def gather(weight):
    stacked = lax.all_gather(weight, "tensor", axis=0)
    groups, rows, columns = stacked.shape
    result = []
    for g in range(groups):
        order = bit_orders()[0 if 2 * g < groups else 1] + [0]
        held, seen = stacked[g], []
        for bit in order:
            other = exchange(held, bit)
            before = 2 ** sum(1 for one in seen if rank(one) > rank(bit))
            shape = (before, held.shape[0] // before, columns)
            held = jnp.stack([held.reshape(shape), other.reshape(shape)], axis=1)
            held = held.reshape(-1, columns)
            seen.append(bit)
        result.append(held)
    return result


def scatter(parts):
    groups = len(parts)
    owned = []
    for g in range(groups):
        order = [0] + bit_orders()[0 if 2 * g < groups else 1][::-1]
        held = parts[g].astype(jnp.bfloat16)
        columns = held.shape[1]
        left = list(order)
        for bit in order:
            before = 2 ** sum(1 for one in left if rank(one) > rank(bit))
            view = held.reshape(before, 2, -1, columns)
            other = exchange(view[:, 1].reshape(-1, columns), bit)
            held = view[:, 0].reshape(-1, columns) + other
            left.remove(bit)
        owned.append(held)
    stacked = jnp.concatenate(owned, axis=0)
    return lax.psum_scatter(stacked, "tensor", scatter_dimension=0, tiled=True).astype(jnp.float32)


def block_sources():
    size = lax.axis_size("dp")
    bits = size.bit_length() - 1
    major = sorted(range(bits), key=rank, reverse=True)
    places = []
    for at in range(size):
        place = 0
        for depth, bit in enumerate(major):
            if (at >> (bits - 1 - depth)) & 1:
                place += 1 << bit
        places.append(place)
    return places


def to_own_order(value):
    me = lax.axis_index("dp")
    places = block_sources()
    axis = value.ndim - 1
    block = value.shape[axis] // len(places)
    return jnp.concatenate(
        [
            lax.dynamic_slice_in_dim(value, jnp.bitwise_xor(me, place) * block, block, axis)
            for place in places
        ],
        axis=axis,
    )


def from_own_order(value):
    me = lax.axis_index("dp")
    places = block_sources()
    slot_of = jnp.array([places.index(i) for i in range(len(places))], jnp.int32)
    axis = value.ndim - 1
    block = value.shape[axis] // len(places)
    return jnp.concatenate(
        [
            lax.dynamic_slice_in_dim(
                value, slot_of[jnp.bitwise_xor(me, i)] * block, block, axis
            )
            for i in range(len(places))
        ],
        axis=axis,
    )


def body(
    tokens,
    lengths,
    w_qkv,
    b_qv,
    w_out,
    b_out,
    gain_one,
    shift_one,
    w_in,
    b_in,
    w_back,
    b_back,
    gain_two,
    shift_two,
    cotangent,
):
    groups = lax.axis_size("tensor")
    slot = lax.axis_index("tensor")
    rows, width = tokens.shape
    seq_len = rows * groups // lengths.shape[0]
    own_seqs = rows // seq_len
    part = w_qkv.shape[2]
    hidden_part = w_in.shape[1]
    head = width // H
    limits = lax.dynamic_slice_in_dim(lengths, slot * own_seqs, own_seqs, 0)

    first = gather(jnp.concatenate([w_qkv.reshape(w_qkv.shape[0], 3 * part), w_out], axis=1))
    full_qkv = [one[:, : 3 * part] for one in first]
    full_out = [one[:, 3 * part :] for one in first]
    full_in = gather(w_in)
    full_back = gather(w_back)
    tokens = to_own_order(tokens)
    cotangent = to_own_order(cotangent)
    vectors = to_own_order(
        jnp.stack([b_out, gain_one, shift_one, b_back, gain_two, shift_two]).astype(jnp.float32)
    )
    b_out, gain_one, shift_one, b_back, gain_two, shift_two = [vectors[i] for i in range(6)]
    bias_qv_all = lax.all_gather(b_qv, "tensor", axis=1, tiled=True).astype(jnp.float32)
    bias_in_all = lax.all_gather(b_in, "tensor", axis=0, tiled=True).astype(jnp.float32)

    qkv_parts = []
    for g in range(groups):
        bias = bias_qv_all[:, g * part : (g + 1) * part]
        bias = jnp.concatenate([bias[0], jnp.zeros((part,), jnp.float32), bias[1]])
        qkv_parts.append((dot(tokens, full_qkv[g]) + bias).astype(jnp.bfloat16))
    qkv = jnp.concatenate(qkv_parts, axis=1)
    attended = attend(limits, qkv, seq_len, part, head)

    attn = sum(
        dot_nt(attended[:, g * part : (g + 1) * part], full_out[g]) for g in range(groups)
    )
    residual_one = tokens.astype(jnp.float32) + attn + b_out.astype(jnp.float32)
    gain_a = gain_one.astype(jnp.float32)
    hidden, scaled_one, inverse_one = normalize(residual_one, gain_a, shift_one.astype(jnp.float32))
    hidden_b = hidden.astype(jnp.bfloat16)

    pre_act = []
    activated = []
    for g in range(groups):
        pre = dot(hidden_b, full_in[g]) + bias_in_all[g * hidden_part : (g + 1) * hidden_part]
        pre_act.append(pre)
        activated.append(jax.nn.gelu(pre, approximate=False).astype(jnp.bfloat16))
    ffn = sum(dot_nt(activated[g], full_back[g]) for g in range(groups))
    residual_two = hidden + ffn + b_back.astype(jnp.float32)
    gain_b = gain_two.astype(jnp.float32)
    output, scaled_two, inverse_two = normalize(residual_two, gain_b, shift_two.astype(jnp.float32))

    grad_out = cotangent.astype(jnp.float32)
    grad_gain_two = jnp.sum(grad_out * scaled_two, axis=0)
    grad_shift_two = jnp.sum(grad_out, axis=0)
    grad_res_two = norm_back(grad_out, scaled_two, inverse_two, gain_b)
    grad_ffn = grad_res_two.astype(jnp.bfloat16)
    grad_b_back = jnp.sum(grad_ffn.astype(jnp.float32), axis=0)
    owner_back = scatter([dot_tn(grad_ffn, activated[g]) for g in range(groups)])

    grad_pre = []
    for g in range(groups):
        pre = pre_act[g]
        slope = 0.5 * (1.0 + lax.erf(pre * SQRT_HALF)) + pre * INV_ROOT_TAU * jnp.exp(
            -0.5 * pre * pre
        )
        grad_pre.append((dot(grad_ffn, full_back[g]) * slope).astype(jnp.bfloat16))
    grad_b_in = jnp.concatenate([jnp.sum(one.astype(jnp.float32), axis=0) for one in grad_pre])
    owner_in = scatter([dot_tn(hidden_b, grad_pre[g]) for g in range(groups)])
    grad_hidden = grad_res_two + sum(dot_nt(grad_pre[g], full_in[g]) for g in range(groups))
    grad_gain_one = jnp.sum(grad_hidden * scaled_one, axis=0)
    grad_shift_one = jnp.sum(grad_hidden, axis=0)
    grad_res_one = norm_back(grad_hidden, scaled_one, inverse_one, gain_a)
    grad_attn = grad_res_one.astype(jnp.bfloat16)
    grad_b_out = jnp.sum(grad_attn.astype(jnp.float32), axis=0)
    owner_out = scatter(
        [dot_tn(grad_attn, attended[:, g * part : (g + 1) * part]) for g in range(groups)]
    )
    grad_mixed = jnp.concatenate(
        [dot(grad_attn, full_out[g]).astype(jnp.bfloat16) for g in range(groups)], axis=1
    )
    grad_qkv = attend_back(limits, qkv, grad_mixed, seq_len, part, head)
    grad_parts = [grad_qkv[:, g * 3 * part : (g + 1) * 3 * part] for g in range(groups)]
    owner_qkv = scatter([dot_tn(tokens, grad_parts[g]) for g in range(groups)])
    grad_tokens = grad_res_one + sum(dot_nt(grad_parts[g], full_qkv[g]) for g in range(groups))
    grad_sums = jnp.sum(grad_qkv.astype(jnp.float32), axis=0).reshape(groups, 3, part)
    grad_b_qv = jnp.stack([grad_sums[:, 0].reshape(width), grad_sums[:, 2].reshape(width)])

    early = from_own_order(
        jnp.stack(
            [
                grad_b_out,
                grad_gain_one,
                grad_shift_one,
                grad_b_back,
                grad_gain_two,
                grad_shift_two,
            ]
        )
    )
    early, late = lax.psum(
        (jnp.concatenate([early, grad_b_in.reshape(-1, width)], axis=0), grad_b_qv),
        ("dp", "tensor"),
    )
    summed = [late, early[6:].reshape(-1)] + [early[i] for i in range(6)]
    owner_b_qv = lax.dynamic_slice_in_dim(summed[0], slot * part, part, 1)
    owner_b_in = lax.dynamic_slice_in_dim(summed[1], slot * hidden_part, hidden_part, 0)
    return (
        from_own_order(output.astype(jnp.bfloat16)),
        from_own_order(grad_tokens),
        owner_qkv.reshape(w_qkv.shape),
        owner_b_qv,
        owner_out,
        summed[2],
        summed[3],
        summed[4],
        owner_in,
        owner_b_in,
        owner_back,
        summed[5],
        summed[6],
        summed[7],
    )


def solution(mesh):
    in_specs = (
        P(("dp", "tensor"), None),
        P("dp"),
        P("dp", None, "tensor"),
        P(None, "tensor"),
        P("dp", "tensor"),
        P(),
        P(),
        P(),
        P("dp", "tensor"),
        P("tensor"),
        P("dp", "tensor"),
        P(),
        P(),
        P(),
        P(("dp", "tensor"), None),
    )
    out_specs = (
        P(("dp", "tensor"), None),
        P(("dp", "tensor"), None),
        P("dp", None, "tensor"),
        P(None, "tensor"),
        P("dp", "tensor"),
        P(),
        P(),
        P(),
        P("dp", "tensor"),
        P("tensor"),
        P("dp", "tensor"),
        P(),
        P(),
        P(),
    )
    return jax.shard_map(body, mesh=mesh, in_specs=in_specs, out_specs=out_specs, check_vma=False)
```

```python
import functools

import jax
import jax.numpy as jnp
from jax import lax
from jax.experimental import pallas as pl
from jax.experimental.pallas import tpu as pltpu
from jax.sharding import PartitionSpec as P

H = 16
EPS = 1e-05
MASKED = -1000000000.0
SQRT_HALF = 0.7071067811865476
INV_ROOT_TAU = 0.3989422804014327
ROWS_NT = (((1,), (1,)), ((), ()))
ROWS_TN = (((0,), (0,)), ((), ()))


def dot(a, b):
    return jnp.dot(a, b, preferred_element_type=jnp.float32)


def dot_nt(a, b):
    return lax.dot_general(a, b, ROWS_NT, preferred_element_type=jnp.float32)


def dot_tn(a, b):
    return lax.dot_general(a, b, ROWS_TN, preferred_element_type=jnp.float32)


def normalize(values, gain, shift):
    centre = values - jnp.mean(values, axis=-1, keepdims=True)
    inverse = lax.rsqrt(jnp.mean(centre * centre, axis=-1, keepdims=True) + EPS)
    scaled = centre * inverse
    return (scaled * gain + shift, scaled, inverse)


def norm_back(grad_out, scaled, inverse, gain):
    grad_scaled = grad_out * gain
    inner = jnp.mean(grad_scaled, axis=-1, keepdims=True)
    along = jnp.mean(grad_scaled * scaled, axis=-1, keepdims=True)
    return inverse * (grad_scaled - inner - scaled * along)


def softmax_of(query, key, limit, scale):
    scores = dot_nt(query, key) * scale
    column = lax.broadcasted_iota(jnp.int32, scores.shape, 1)
    scores = jnp.where(column < limit, scores, MASKED)
    expo = jnp.exp(scores - jnp.max(scores, axis=-1, keepdims=True))
    return expo * (1.0 / jnp.sum(expo, axis=-1, keepdims=True))


def attend_kernel(width, head, seq_len, limit_ref, qkv_ref, out_ref):
    limit = limit_ref[pl.program_id(0)]
    for at in range(width // head):
        low = at * head
        query = qkv_ref[:, low : low + head]
        key = qkv_ref[:, width + low : width + low + head]
        value = qkv_ref[:, 2 * width + low : 2 * width + low + head]
        probs = softmax_of(query, key, limit, head**-0.5).astype(jnp.bfloat16)
        out_ref[:, low : low + head] = dot(probs, value).astype(jnp.bfloat16)


def attend_back_kernel(width, head, seq_len, limit_ref, qkv_ref, grad_ref, out_ref):
    limit = limit_ref[pl.program_id(0)]
    scale = head**-0.5
    for at in range(width // head):
        low = at * head
        query = qkv_ref[:, low : low + head]
        key = qkv_ref[:, width + low : width + low + head]
        value = qkv_ref[:, 2 * width + low : 2 * width + low + head]
        grad = grad_ref[:, low : low + head]
        probs = softmax_of(query, key, limit, scale)
        grad_probs = dot_nt(grad, value)
        inner = jnp.sum(grad_probs * probs, axis=-1, keepdims=True)
        grad_scores = (probs * (grad_probs - inner)).astype(jnp.bfloat16)
        out_ref[:, low : low + head] = (dot(grad_scores, key) * scale).astype(jnp.bfloat16)
        out_ref[:, width + low : width + low + head] = (dot_tn(grad_scores, query) * scale).astype(
            jnp.bfloat16
        )
        out_ref[:, 2 * width + low : 2 * width + low + head] = dot_tn(
            probs.astype(jnp.bfloat16), grad
        ).astype(jnp.bfloat16)


def attend(limits, qkv, seq_len, width, head):
    rows = qkv.shape[0]
    groups = qkv.shape[1] // (3 * width)
    return pl.pallas_call(
        functools.partial(attend_kernel, width, head, seq_len),
        grid_spec=pltpu.PrefetchScalarGridSpec(
            num_scalar_prefetch=1,
            grid=(rows // seq_len, groups),
            in_specs=[pl.BlockSpec((seq_len, 3 * width), lambda s, g, lim: (s, g))],
            out_specs=pl.BlockSpec((seq_len, width), lambda s, g, lim: (s, g)),
        ),
        out_shape=jax.ShapeDtypeStruct((rows, groups * width), jnp.bfloat16),
        cost_estimate=pl.CostEstimate(
            flops=16 * rows * seq_len * groups * width,
            bytes_accessed=8 * rows * groups * width,
            transcendentals=rows * seq_len * groups * width // head,
        ),
    )(limits, qkv)


def attend_back(limits, qkv, grad, seq_len, width, head):
    rows = qkv.shape[0]
    groups = qkv.shape[1] // (3 * width)
    return pl.pallas_call(
        functools.partial(attend_back_kernel, width, head, seq_len),
        grid_spec=pltpu.PrefetchScalarGridSpec(
            num_scalar_prefetch=1,
            grid=(rows // seq_len, groups),
            in_specs=[
                pl.BlockSpec((seq_len, 3 * width), lambda s, g, lim: (s, g)),
                pl.BlockSpec((seq_len, width), lambda s, g, lim: (s, g)),
            ],
            out_specs=pl.BlockSpec((seq_len, 3 * width), lambda s, g, lim: (s, g)),
        ),
        out_shape=jax.ShapeDtypeStruct(qkv.shape, jnp.bfloat16),
        cost_estimate=pl.CostEstimate(
            flops=40 * rows * seq_len * groups * width,
            bytes_accessed=14 * rows * groups * width,
            transcendentals=rows * seq_len * groups * width // head,
        ),
    )(limits, qkv, grad)


def bit_orders():
    bits = lax.axis_size("dp").bit_length() - 1
    outer = list(range(1, bits))
    return outer, outer[::-1]


def exchange(value, bit):
    size = lax.axis_size("dp")
    return lax.ppermute(value, "dp", [(i, i ^ (1 << bit)) for i in range(size)])


def rank(bit):
    return lax.axis_size("dp") if bit == 0 else bit


def gather(weight):
    stacked = lax.all_gather(weight, "tensor", axis=0)
    groups, rows, columns = stacked.shape
    result = []
    for g in range(groups):
        order = bit_orders()[0 if 2 * g < groups else 1] + [0]
        held, seen = stacked[g], []
        for bit in order:
            other = exchange(held, bit)
            before = 2 ** sum(1 for one in seen if rank(one) > rank(bit))
            shape = (before, held.shape[0] // before, columns)
            held = jnp.stack([held.reshape(shape), other.reshape(shape)], axis=1)
            held = held.reshape(-1, columns)
            seen.append(bit)
        result.append(held)
    return result


def scatter(parts):
    groups = len(parts)
    owned = []
    for g in range(groups):
        order = [0] + bit_orders()[0 if 2 * g < groups else 1][::-1]
        held = parts[g].astype(jnp.bfloat16)
        columns = held.shape[1]
        left = list(order)
        for bit in order:
            before = 2 ** sum(1 for one in left if rank(one) > rank(bit))
            view = held.reshape(before, 2, -1, columns)
            other = exchange(view[:, 1].reshape(-1, columns), bit)
            held = view[:, 0].reshape(-1, columns) + other
            left.remove(bit)
        owned.append(held)
    stacked = jnp.concatenate(owned, axis=0)
    return lax.psum_scatter(stacked, "tensor", scatter_dimension=0, tiled=True).astype(jnp.float32)


def block_sources():
    size = lax.axis_size("dp")
    bits = size.bit_length() - 1
    major = sorted(range(bits), key=rank, reverse=True)
    places = []
    for at in range(size):
        place = 0
        for depth, bit in enumerate(major):
            if (at >> (bits - 1 - depth)) & 1:
                place += 1 << bit
        places.append(place)
    return places


def to_own_order(value):
    me = lax.axis_index("dp")
    places = block_sources()
    axis = value.ndim - 1
    block = value.shape[axis] // len(places)
    return jnp.concatenate(
        [
            lax.dynamic_slice_in_dim(value, jnp.bitwise_xor(me, place) * block, block, axis)
            for place in places
        ],
        axis=axis,
    )


def from_own_order(value):
    me = lax.axis_index("dp")
    places = block_sources()
    slot_of = jnp.array([places.index(i) for i in range(len(places))], jnp.int32)
    axis = value.ndim - 1
    block = value.shape[axis] // len(places)
    return jnp.concatenate(
        [
            lax.dynamic_slice_in_dim(
                value, slot_of[jnp.bitwise_xor(me, i)] * block, block, axis
            )
            for i in range(len(places))
        ],
        axis=axis,
    )


def body(
    tokens,
    lengths,
    w_qkv,
    b_qv,
    w_out,
    b_out,
    gain_one,
    shift_one,
    w_in,
    b_in,
    w_back,
    b_back,
    gain_two,
    shift_two,
    cotangent,
):
    groups = lax.axis_size("tensor")
    slot = lax.axis_index("tensor")
    rows, width = tokens.shape
    seq_len = rows * groups // lengths.shape[0]
    own_seqs = rows // seq_len
    part = w_qkv.shape[2]
    hidden_part = w_in.shape[1]
    head = width // H
    limits = lax.dynamic_slice_in_dim(lengths, slot * own_seqs, own_seqs, 0)

    first = gather(jnp.concatenate([w_qkv.reshape(w_qkv.shape[0], 3 * part), w_out], axis=1))
    full_qkv = [one[:, : 3 * part] for one in first]
    full_out = [one[:, 3 * part :] for one in first]
    full_in = gather(w_in)
    full_back = gather(w_back)
    tokens = to_own_order(tokens)
    cotangent = to_own_order(cotangent)
    vectors = to_own_order(
        jnp.stack([b_out, gain_one, shift_one, b_back, gain_two, shift_two]).astype(jnp.float32)
    )
    b_out, gain_one, shift_one, b_back, gain_two, shift_two = [vectors[i] for i in range(6)]
    biases = lax.all_gather(jnp.concatenate([b_qv.reshape(-1), b_in]), "tensor", axis=0)
    biases = biases.astype(jnp.float32)
    bias_qv_all = jnp.concatenate(
        [biases[g, : 2 * part].reshape(2, part) for g in range(groups)], axis=1
    )
    bias_in_all = biases[:, 2 * part :].reshape(-1)

    qkv_parts = []
    for g in range(groups):
        bias = bias_qv_all[:, g * part : (g + 1) * part]
        bias = jnp.concatenate([bias[0], jnp.zeros((part,), jnp.float32), bias[1]])
        qkv_parts.append((dot(tokens, full_qkv[g]) + bias).astype(jnp.bfloat16))
    qkv = jnp.concatenate(qkv_parts, axis=1)
    attended = attend(limits, qkv, seq_len, part, head)

    attn = sum(
        dot_nt(attended[:, g * part : (g + 1) * part], full_out[g]) for g in range(groups)
    )
    residual_one = tokens.astype(jnp.float32) + attn + b_out.astype(jnp.float32)
    gain_a = gain_one.astype(jnp.float32)
    hidden, scaled_one, inverse_one = normalize(residual_one, gain_a, shift_one.astype(jnp.float32))
    hidden_b = hidden.astype(jnp.bfloat16)

    pre_act = []
    activated = []
    for g in range(groups):
        pre = dot(hidden_b, full_in[g]) + bias_in_all[g * hidden_part : (g + 1) * hidden_part]
        pre_act.append(pre)
        activated.append(jax.nn.gelu(pre, approximate=False).astype(jnp.bfloat16))
    ffn = sum(dot_nt(activated[g], full_back[g]) for g in range(groups))
    residual_two = hidden + ffn + b_back.astype(jnp.float32)
    gain_b = gain_two.astype(jnp.float32)
    output, scaled_two, inverse_two = normalize(residual_two, gain_b, shift_two.astype(jnp.float32))

    grad_out = cotangent.astype(jnp.float32)
    grad_gain_two = jnp.sum(grad_out * scaled_two, axis=0)
    grad_shift_two = jnp.sum(grad_out, axis=0)
    grad_res_two = norm_back(grad_out, scaled_two, inverse_two, gain_b)
    grad_ffn = grad_res_two.astype(jnp.bfloat16)
    grad_b_back = jnp.sum(grad_ffn.astype(jnp.float32), axis=0)
    owner_back = scatter([dot_tn(grad_ffn, activated[g]) for g in range(groups)])

    grad_pre = []
    for g in range(groups):
        pre = pre_act[g]
        slope = 0.5 * (1.0 + lax.erf(pre * SQRT_HALF)) + pre * INV_ROOT_TAU * jnp.exp(
            -0.5 * pre * pre
        )
        grad_pre.append((dot(grad_ffn, full_back[g]) * slope).astype(jnp.bfloat16))
    grad_b_in = jnp.concatenate([jnp.sum(one.astype(jnp.float32), axis=0) for one in grad_pre])
    owner_in = scatter([dot_tn(hidden_b, grad_pre[g]) for g in range(groups)])
    grad_hidden = grad_res_two + sum(dot_nt(grad_pre[g], full_in[g]) for g in range(groups))
    grad_gain_one = jnp.sum(grad_hidden * scaled_one, axis=0)
    grad_shift_one = jnp.sum(grad_hidden, axis=0)
    grad_res_one = norm_back(grad_hidden, scaled_one, inverse_one, gain_a)
    grad_attn = grad_res_one.astype(jnp.bfloat16)
    grad_b_out = jnp.sum(grad_attn.astype(jnp.float32), axis=0)
    owner_out = scatter(
        [dot_tn(grad_attn, attended[:, g * part : (g + 1) * part]) for g in range(groups)]
    )
    grad_mixed = jnp.concatenate(
        [dot(grad_attn, full_out[g]).astype(jnp.bfloat16) for g in range(groups)], axis=1
    )
    grad_qkv = attend_back(limits, qkv, grad_mixed, seq_len, part, head)
    grad_parts = [grad_qkv[:, g * 3 * part : (g + 1) * 3 * part] for g in range(groups)]
    owner_qkv = scatter([dot_tn(tokens, grad_parts[g]) for g in range(groups)])
    grad_tokens = grad_res_one + sum(dot_nt(grad_parts[g], full_qkv[g]) for g in range(groups))
    grad_sums = jnp.sum(grad_qkv.astype(jnp.float32), axis=0).reshape(groups, 3, part)
    grad_b_qv = jnp.stack([grad_sums[:, 0].reshape(width), grad_sums[:, 2].reshape(width)])

    early = from_own_order(
        jnp.stack(
            [
                grad_b_out,
                grad_gain_one,
                grad_shift_one,
                grad_b_back,
                grad_gain_two,
                grad_shift_two,
            ]
        )
    )
    early, late = lax.psum(
        (jnp.concatenate([early, grad_b_in.reshape(-1, width)], axis=0), grad_b_qv),
        ("dp", "tensor"),
    )
    summed = [late, early[6:].reshape(-1)] + [early[i] for i in range(6)]
    owner_b_qv = lax.dynamic_slice_in_dim(summed[0], slot * part, part, 1)
    owner_b_in = lax.dynamic_slice_in_dim(summed[1], slot * hidden_part, hidden_part, 0)
    return (
        from_own_order(output.astype(jnp.bfloat16)),
        from_own_order(grad_tokens),
        owner_qkv.reshape(w_qkv.shape),
        owner_b_qv,
        owner_out,
        summed[2],
        summed[3],
        summed[4],
        owner_in,
        owner_b_in,
        owner_back,
        summed[5],
        summed[6],
        summed[7],
    )


def solution(mesh):
    in_specs = (
        P(("dp", "tensor"), None),
        P("dp"),
        P("dp", None, "tensor"),
        P(None, "tensor"),
        P("dp", "tensor"),
        P(),
        P(),
        P(),
        P("dp", "tensor"),
        P("tensor"),
        P("dp", "tensor"),
        P(),
        P(),
        P(),
        P(("dp", "tensor"), None),
    )
    out_specs = (
        P(("dp", "tensor"), None),
        P(("dp", "tensor"), None),
        P("dp", None, "tensor"),
        P(None, "tensor"),
        P("dp", "tensor"),
        P(),
        P(),
        P(),
        P("dp", "tensor"),
        P("tensor"),
        P("dp", "tensor"),
        P(),
        P(),
        P(),
    )
    return jax.shard_map(body, mesh=mesh, in_specs=in_specs, out_specs=out_specs, check_vma=False)
```
